32 devices in a mesh: shard: 4 (over y, x), context: 4 (over z), tensor: 2 (over core).
Axes of the slice: x: 2, y: 2, z: 4, core: 2. Of those that a mesh axis runs over, the one named last changes fastest.
Arguments:
- tokens: bfloat16 [12, 1024, 768], P('shard', 'context'), may hold values from -6 to 6
- lengths: int32 [12], P('shard'), may hold values from 256 to 1024, as said below
- cotangent: bfloat16 [12, 1024, 768], P('shard', 'context'), may hold values from -6 to 6
- norm_attn: bfloat16 [768], P('shard'), may hold values from 0.099609375 to 1.8984375
- w_query: bfloat16 [768, 768], P('shard', 'tensor'), may hold values from -0.02734375 to 0.02734375
- w_key: bfloat16 [768, 768], P('shard', 'tensor'), may hold values from -0.21875 to 0.21875
- w_value: bfloat16 [768, 768], P('shard', 'tensor'), may hold values from -0.21875 to 0.21875
- w_attn_out: bfloat16 [768, 768], P('tensor', 'shard'), may hold values from -1.25 to 1.25
- bias_table: bfloat16 [32, 12], P('shard', 'tensor'), may hold values from -4 to 4
- norm_ffn: bfloat16 [768], P('shard'), may hold values from 0.099609375 to 1.8984375
- w_ffn_in: bfloat16 [768, 3072], P('shard', 'tensor'), may hold values from -0.21875 to 0.21875
- w_ffn_out: bfloat16 [3072, 768], P('tensor', 'shard'), may hold values from -0.109375 to 0.109375
Outputs:
- out: bfloat16 [12, 1024, 768], P('shard', 'context')
- grad_tokens: float32 [12, 1024, 768], P('shard', 'context')
- grad_norm_attn: float32 [768], P('shard')
- grad_w_query: float32 [768, 768], P('shard', 'tensor')
- grad_w_key: float32 [768, 768], P('shard', 'tensor')
- gradient_value_weight: float32 [768, 768], P('shard', 'tensor')
- grad_w_attn_out: float32 [768, 768], P('tensor', 'shard')
- gradient_bias_lookup: float32 [32, 12], P('shard', 'tensor')
- grad_norm_ffn: float32 [768], P('shard')
- grad_w_ffn_in: float32 [768, 3072], P('shard', 'tensor')
- grad_w_ffn_out: float32 [3072, 768], P('tensor', 'shard')
The draws below stay inside these ranges and needn't reach their ends.
Inputs may be any that keep to these rules, and one draw needn't show every extreme that they name: A slot's valid tokens are its first lengths[s] positions. Some slot holds exactly 1024 and some exactly 256.
All inputs are finite; a program needn't handle non-finite values.
Results may differ from the reference program's by a relative error of at most 0.028.
Values may be sent and summed in bfloat16 or wider, within the bound.
No kernel may reach another device: no remote copies, remote signals or barrier semaphores. Data moves between devices by JAX's collectives and lax.ppermute only.
A program may use at most 256 MiB of HBM per device.

```python
import jax
import jax.numpy as jnp
from jax import lax

D = 768
H = 12
HD = 64
FF = 3072
NB = 32
L = 1024
SLOTS = 12


def draw_lengths(key, part):
    key_one, key_two = jax.random.split(key)
    lengths_drawn = jax.random.randint(key_one, (SLOTS,), L // 4, L + 1)
    shuffled = jax.random.permutation(key_two, SLOTS)
    lengths_drawn = lengths_drawn.at[shuffled[0]].set(L)
    lengths_drawn = lengths_drawn.at[shuffled[1]].set(L // 4)
    return lengths_drawn.astype(jnp.int32)


def shard_levels(rng, shape, cuts, low, top_value):
    factor_of, own = 1.0, jax.random.fold_in(rng, 6)
    for position, parts in cuts:
        steps = jnp.exp(jax.random.uniform(jax.random.fold_in(own, position), (parts,), jnp.float32, low / len(cuts), top_value / len(cuts)))
        factor_of = factor_of * jnp.repeat(steps, shape[position] // parts).reshape([-1 if axis == position else 1 for axis in range(len(shape))])
    return factor_of


def gaussian(key, shape, deviation, bound, shards=(), held_as=jnp.bfloat16):
    drawn = jax.random.normal(key, shape, jnp.float32) * deviation
    if len(shards) > 0:
        drawn = shard_levels(key, shape, shards, -0.22, 0.18) * drawn
    return jnp.clip(drawn, min=-bound, max=bound).astype(held_as)


def setup_inputs(seed: int = 0) -> dict:
    key_of = jax.random.split(jax.random.key(seed), 13)
    return {
        "tokens": gaussian(key_of[0], (SLOTS, L, D), 1.0, 6.0, ((0, 4), (1, 4))),
        "lengths": draw_lengths(jax.random.fold_in(key_of[12], 71), 0),
        "cotangent": gaussian(key_of[2], (SLOTS, L, D), 1.0, 6.0, ((0, 4), (1, 4))),
        "norm_attn": jnp.clip(1.0 + 0.18 * jax.random.normal(key_of[3], (D,), jnp.float32), 0.099609375, 1.8984375).astype(jnp.bfloat16),
        "w_query": gaussian(key_of[4], (D, D), (D * HD) ** -0.5, 0.02734375, ((0, 4), (1, 2))),
        "w_key": gaussian(key_of[5], (D, D), D ** -0.5, 0.21875, ((0, 4), (1, 2))),
        "w_value": gaussian(key_of[6], (D, D), D ** -0.5, 0.21875, ((0, 4), (1, 2))),
        "w_attn_out": gaussian(key_of[7], (D, D), (max(D // 32, 1)) ** -0.5, 1.25, ((0, 2), (1, 4))),
        "bias_table": gaussian(key_of[8], (NB, H), 1.0, 4.0, ((0, 4), (1, 2))),
        "norm_ffn": jnp.clip(1.0 + 0.18 * jax.random.normal(key_of[9], (D,), jnp.float32), 0.099609375, 1.8984375).astype(jnp.bfloat16),
        "w_ffn_in": gaussian(key_of[10], (D, FF), D ** -0.5, 0.21875, ((0, 4), (1, 2))),
        "w_ffn_out": gaussian(key_of[11], (FF, D), FF ** -0.5, 0.109375, ((0, 2), (1, 4))),
    }


@jax.custom_vjp
def low(v):
    return lax.optimization_barrier(v.astype(jnp.bfloat16)).astype(jnp.float32)

@jax.custom_vjp
def low_back(v):
    return v

def low_keep(v):
    return (low(v), None)

def low_pass(kept, grad):
    return (grad,)

def back_keep(v):
    return (v, None)

def back_low(kept, grad):
    return (low(grad),)
low.defvjp(low_keep, low_pass)
low_back.defvjp(back_keep, back_low)
boundaries = (12, 16, 23, 32, 46, 64, 91)
eps_norm = 1e-06
masked_score = -1000000000.0
highest = lax.Precision.HIGHEST

def gelu_tanh(value):
    return 0.5 * value * (1.0 + jnp.tanh(0.7978845608028654 * (value + 0.044715 * value * value * value)))

def bucket_full(length):
    positions = jnp.arange(length, dtype=jnp.int32)
    relative = positions[None, :] - positions[:, None]
    distance = jnp.abs(relative)
    bucket_idx = 16 * (relative > 0).astype(jnp.int32) + jnp.minimum(distance, 8)
    for boundary in boundaries:
        bucket_idx = bucket_idx + (distance >= boundary).astype(jnp.int32)
    return bucket_idx

def rms_norm(stream, gain):
    return stream * lax.rsqrt(lax.optimization_barrier(jnp.mean(stream * stream, axis=-1, keepdims=True)) + eps_norm) * gain

def block(stream, params, bucket_idx, key_valid):
    norm_attn, w_query, w_key, w_value, w_attn_out, bias_table, norm_ffn, w_ffn_in, w_ffn_out = params
    head_count = bias_table.shape[1]
    head_dim = w_query.shape[1] // head_count
    normed_one = low(rms_norm(stream, norm_attn))
    queries = low(low_back(jnp.dot(normed_one, w_query, precision=highest))).reshape(-1, head_count, head_dim)
    keys_all = low(low_back(jnp.dot(normed_one, w_key, precision=highest))).reshape(-1, head_count, head_dim)
    values_all = low(low_back(jnp.dot(normed_one, w_value, precision=highest))).reshape(-1, head_count, head_dim)
    raw_scores = jnp.einsum('qhd,khd->hqk', queries, keys_all, precision=highest)
    raw_scores = raw_scores + jnp.transpose(bias_table[bucket_idx], (2, 0, 1))
    scores = low_back(jnp.where(key_valid[None, None, :], raw_scores, masked_score))
    attn_probs = jax.nn.softmax(scores, axis=-1)
    context = jnp.einsum('hqk,khd->qhd', low(attn_probs), values_all, precision=highest)
    context = low(low_back(context)).reshape(-1, head_count * head_dim)
    attn_branch = low_back(jnp.dot(context, w_attn_out, precision=highest))
    middle = stream + attn_branch
    normed_two = low(rms_norm(middle, norm_ffn))
    pre_act = low_back(jnp.dot(normed_two, w_ffn_in, precision=highest))
    hidden_state = low(gelu_tanh(pre_act))
    ffn_branch = low_back(jnp.dot(hidden_state, w_ffn_out, precision=highest))
    return middle + ffn_branch

def tower(stream, length, params, bucket_idx):
    key_valid = jnp.arange(L, dtype=jnp.int32) < length
    first_out = block(stream, params, bucket_idx, key_valid)
    second_out = block(first_out, params, bucket_idx, key_valid)
    return jnp.where(key_valid[:, None], second_out, 0.0)

def forward(tokens32, params, lengths, bucket_idx):

    def scan_step(carried, element):
        stream, length = element
        return (carried, jax.checkpoint(tower)(stream, length, params, bucket_idx))
    unused_carry, outputs = lax.scan(scan_step, jnp.zeros((), jnp.float32), (tokens32, lengths))
    return outputs

def reference(tokens, lengths, cotangent, norm_attn, w_query, w_key, w_value, w_attn_out, bias_table, norm_ffn, w_ffn_in, w_ffn_out):
    params = tuple((weight.astype(jnp.float32) for weight in (norm_attn, w_query, w_key, w_value, w_attn_out, bias_table, norm_ffn, w_ffn_in, w_ffn_out)))
    bucket_idx = bucket_full(L)

    def whole_net(tokens32, params32):
        return forward(tokens32, params32, lengths, bucket_idx)
    result, pullback = jax.vjp(whole_net, tokens.astype(jnp.float32), params)
    grad_tokens, grad_params = pullback(cotangent.astype(jnp.float32))
    return (result.astype(jnp.bfloat16), grad_tokens, grad_params[0], grad_params[1], grad_params[2], grad_params[3], grad_params[4], grad_params[5], grad_params[6], grad_params[7], grad_params[8])
```

```python
import functools

import jax
import jax.numpy as jnp
from jax import lax
from jax.experimental import pallas as pl
from jax.experimental.pallas import tpu as pltpu
from jax.sharding import PartitionSpec as P

NB = 32
LANES = 128
boundaries = (12, 16, 23, 32, 46, 64, 91)
eps_norm = 1e-06
masked_score = -1000000000.0
bf16 = jnp.bfloat16
f32 = jnp.float32
NT = (((1,), (1,)), ((), ()))
TN = (((0,), (0,)), ((), ()))
NN = (((1,), (0,)), ((), ()))


def mm(left, right, dims=NN):
    return lax.dot_general(left, right, dims, preferred_element_type=f32)


def bucket_of(relative):
    distance = jnp.abs(relative)
    bucket_idx = 16 * (relative > 0).astype(jnp.int32) + jnp.minimum(distance, 8)
    for boundary in boundaries:
        bucket_idx = bucket_idx + (distance >= boundary).astype(jnp.int32)
    return bucket_idx


def whole(shape):
    zeros = (0,) * len(shape)
    return pl.BlockSpec(shape, lambda *_: zeros)


SMEM_SPEC = pl.BlockSpec(memory_space=pltpu.SMEM)


def call(kernel, grid, in_specs, out_specs, out_shapes, scratch=(), vmem=48):
    return pl.pallas_call(
        kernel,
        grid=grid,
        in_specs=in_specs,
        out_specs=out_specs,
        out_shape=out_shapes,
        scratch_shapes=list(scratch),
        compiler_params=pltpu.CompilerParams(
            vmem_limit_bytes=vmem * 1024 * 1024,
            dimension_semantics=("arbitrary",) * len(grid),
        ),
    )


def row_scale(stream):
    return lax.rsqrt(jnp.mean(stream * stream, axis=-1, keepdims=True) + eps_norm)


def norm_back(stream, gain, grad_normed):
    scale = row_scale(stream)
    scaled = gain * grad_normed
    inner = jnp.mean(stream * scaled, axis=-1, keepdims=True)
    unit = stream * scale
    grad_gain = jnp.sum(unit * grad_normed, axis=0, keepdims=True)
    return scale * scaled - unit * (scale * scale * inner), grad_gain


def bias_kernel(vec_ref, out_ref, *, rows, total):
    width = vec_ref.shape[-1]
    spread = jnp.broadcast_to(vec_ref[0], (rows, width))
    rolled = pltpu.roll(spread, width - (rows - 1), 1, stride=1, stride_axis=0)
    out_ref[0] = rolled[:, :total].astype(bf16)


def bias_tile(vec, rows, total):
    heads, width = vec.shape
    return call(
        functools.partial(bias_kernel, rows=rows, total=total),
        (heads,),
        [pl.BlockSpec((1, 1, width), lambda h: (h, 0, 0))],
        pl.BlockSpec((1, rows, total), lambda h: (h, 0, 0)),
        jax.ShapeDtypeStruct((heads, rows, total), bf16),
    )(vec.reshape(heads, 1, width))


def attn_fwd_kernel(*refs, pieces, rows, inner, raw):
    sc = refs[0]
    mine = refs[1 : 1 + pieces]
    other = refs[1 + pieces : 1 + 2 * pieces]
    gain, w_ref, bias_ref = refs[1 + 2 * pieces : 4 + 2 * pieces]
    n1_ref, q_ref, kv_ref, e_ref, c32_ref, rl_ref, c_ref, a_ref = refs[4 + 2 * pieces :]
    half = rows // 2
    total = rows * pieces
    step = pl.program_id(0)
    block = sc[0]
    core = sc[1]
    length = sc[2]

    @pl.when(step == 0)
    def _():
        for side, group in ((core, mine), (1 - core, other)):
            for k in range(pieces):
                value = group[k][...]
                if raw:
                    value = value.astype(f32)
                    value = (value * row_scale(value) * gain[...]).astype(bf16)
                start = pl.multiple_of((block ^ k) * rows + side * half, half)
                n1_ref[pl.ds(start, half), :] = value
        kv_ref[...] = mm(n1_ref[...], w_ref[:, inner : 3 * inner]).astype(bf16)
        own = n1_ref[pl.ds(pl.multiple_of(block * rows, rows), rows), :]
        q_ref[...] = mm(own, w_ref[:, :inner]).astype(bf16)

    lane = pl.multiple_of(step * LANES, LANES)
    low = lax.broadcasted_iota(jnp.int32, (rows, LANES), 1) < LANES // 2
    queries = q_ref[:, pl.ds(lane, LANES)]
    keys = kv_ref[:, pl.ds(lane, LANES)]
    values = kv_ref[:, pl.ds(pl.multiple_of(inner + step * LANES, LANES), LANES)]
    values = jnp.concatenate([values, jnp.ones_like(values)], axis=1)
    key_pos = lax.broadcasted_iota(jnp.int32, (1, total), 1)
    mask_row = jnp.where(key_pos < length, 0.0, masked_score)
    parts = []
    for h in range(2):
        picked = jnp.where(low if h == 0 else ~low, queries, jnp.zeros_like(queries))
        scores = mm(picked, keys, NT) + bias_ref[h].astype(f32) + mask_row
        top = jnp.max(scores, axis=-1, keepdims=True)
        weights = jnp.exp(scores - top).astype(bf16)
        e_ref[h] = weights
        summed = mm(weights, values)
        inverse = 1.0 / summed[:, LANES:]
        parts.append((summed[:, :LANES] * inverse, inverse))
    context = jnp.where(low, parts[0][0], parts[1][0])
    c32_ref[:, pl.ds(lane, LANES)] = context
    rl_ref[:, pl.ds(lane, LANES)] = jnp.where(low, parts[0][1], parts[1][1])
    c_ref[:, pl.ds(lane, LANES)] = context.astype(bf16)

    @pl.when(step == pl.num_programs(0) - 1)
    def _():
        a_ref[...] = mm(c_ref[...], w_ref[:, 3 * inner : 4 * inner], NT).astype(bf16)


def attn_fwd(sc, mine, other, gain, w1, bias, raw):
    pieces = len(mine)
    half, width = mine[0].shape
    rows = 2 * half
    total = rows * pieces
    heads = bias.shape[0]
    inner = heads * 64
    shapes = [
        ((total, width), bf16),
        ((rows, inner), bf16),
        ((total, 2 * inner), bf16),
        ((heads, rows, total), bf16),
        ((rows, inner), f32),
        ((rows, inner), f32),
        ((rows, inner), bf16),
        ((rows, width), bf16),
    ]
    pair = pl.BlockSpec((2, rows, total), lambda p: (p, 0, 0))
    out_specs = [whole(s) for s, _ in shapes]
    out_specs[3] = pair
    return call(
        functools.partial(attn_fwd_kernel, pieces=pieces, rows=rows, inner=inner, raw=raw),
        (heads // 2,),
        [SMEM_SPEC]
        + [whole((half, width))] * (2 * pieces)
        + [whole(gain.shape), whole(w1.shape), pair],
        out_specs,
        [jax.ShapeDtypeStruct(s, d) for s, d in shapes],
    )(sc, *mine, *other, gain, w1, bias)


def gelu_parts(value):
    squared = value * value
    inside = 0.7978845608028654 * value * (1.0 + 0.044715 * squared)
    tanh = jnp.tanh(inside)
    half_up = 0.5 * (1.0 + tanh)
    slope = half_up + 0.5 * value * (1.0 - tanh * tanh) * (
        0.7978845608028654 * (1.0 + 3.0 * 0.044715 * squared)
    )
    return value * half_up, slope


def ffn_fwd_kernel(
    x_ref, own, oth, gain, wi, wo, m_ref, n2_ref, r_ref, gp_ref, b_ref, acc_ref
):
    step = pl.program_id(0)

    @pl.when(step == 0)
    def _():
        middle = x_ref[...] + (own[...].astype(f32) + oth[...].astype(f32))
        m_ref[...] = middle
        n2_ref[...] = (middle * row_scale(middle) * gain[...]).astype(bf16)
        acc_ref[...] = jnp.zeros_like(acc_ref)

    act, slope = gelu_parts(mm(n2_ref[...], wi[...]))
    act = act.astype(bf16)
    r_ref[...] = act
    gp_ref[...] = slope.astype(bf16)
    acc_ref[...] += mm(act, wo[...], NT)

    @pl.when(step == pl.num_programs(0) - 1)
    def _():
        b_ref[...] = acc_ref[...].astype(bf16)


def ffn_specs(rows, width, hidden, chunk):
    count = hidden // chunk
    stream = whole((rows, width))
    first = pl.BlockSpec((width, chunk), lambda j: (0, j))
    second = pl.BlockSpec((width, chunk), lambda j: (0, j + count))
    part = pl.BlockSpec((rows, chunk), lambda j: (0, j))
    return count, stream, first, second, part


def ffn_fwd(x, own, oth, gain, w2, chunk=512):
    rows, width = x.shape
    hidden = w2.shape[1] // 2
    count, stream, first, second, part = ffn_specs(rows, width, hidden, chunk)
    return call(
        ffn_fwd_kernel,
        (count,),
        [stream, stream, stream, whole(gain.shape), first, second],
        [stream, stream, part, part, stream],
        [
            jax.ShapeDtypeStruct((rows, width), f32),
            jax.ShapeDtypeStruct((rows, width), bf16),
            jax.ShapeDtypeStruct((rows, hidden), bf16),
            jax.ShapeDtypeStruct((rows, hidden), bf16),
            jax.ShapeDtypeStruct((rows, width), bf16),
        ],
        [pltpu.VMEM((rows, width), f32)],
    )(x, own, oth, gain, w2, w2)


def ffn_both_kernel(
    x_ref, own, oth, gain, df_ref, wi, wo,
    m_ref, n2_ref, r_ref, du_ref, b_ref, dn_ref, acc_ref, dacc_ref,
):
    step = pl.program_id(0)

    @pl.when(step == 0)
    def _():
        middle = x_ref[...] + (own[...].astype(f32) + oth[...].astype(f32))
        m_ref[...] = middle
        n2_ref[...] = (middle * row_scale(middle) * gain[...]).astype(bf16)
        acc_ref[...] = jnp.zeros_like(acc_ref)
        dacc_ref[...] = jnp.zeros_like(dacc_ref)

    act, slope = gelu_parts(mm(n2_ref[...], wi[...]))
    act = act.astype(bf16)
    r_ref[...] = act
    acc_ref[...] += mm(act, wo[...], NT)
    du = (mm(df_ref[...], wo[...]) * slope).astype(bf16)
    du_ref[...] = du
    dacc_ref[...] += mm(du, wi[...], NT)

    @pl.when(step == pl.num_programs(0) - 1)
    def _():
        b_ref[...] = acc_ref[...].astype(bf16)
        dn_ref[...] = dacc_ref[...].astype(bf16)


def ffn_both(x, own, oth, gain, df, w2, chunk=512):
    rows, width = x.shape
    hidden = w2.shape[1] // 2
    count, stream, first, second, part = ffn_specs(rows, width, hidden, chunk)
    return call(
        ffn_both_kernel,
        (count,),
        [stream, stream, stream, whole(gain.shape), stream, first, second],
        [stream, stream, part, part, stream, stream],
        [
            jax.ShapeDtypeStruct((rows, width), f32),
            jax.ShapeDtypeStruct((rows, width), bf16),
            jax.ShapeDtypeStruct((rows, hidden), bf16),
            jax.ShapeDtypeStruct((rows, hidden), bf16),
            jax.ShapeDtypeStruct((rows, width), bf16),
            jax.ShapeDtypeStruct((rows, width), bf16),
        ],
        [pltpu.VMEM((rows, width), f32)] * 2,
    )(x, own, oth, gain, df, w2, w2)


def join_halves(sc, mine, other, joined):
    part = mine.shape[0]
    core = sc[1]
    joined[pl.ds(pl.multiple_of(core * part, part), part), :] = mine[...].astype(f32)
    joined[pl.ds(pl.multiple_of((1 - core) * part, part), part), :] = other[...].astype(f32)
    return joined[...].T


def ffn_bwd_kernel(
    sc, x_ref, dm_ref, mine, other, gain, r_ref, gp_ref, wi, wo,
    g_ref, df_ref, du_ref, dn_ref, gg_ref, joined, dacc_ref,
):
    step = pl.program_id(0)

    @pl.when(step == 0)
    def _():
        grad, grad_gain = norm_back(x_ref[...], gain[...], join_halves(sc, mine, other, joined))
        grad = grad + dm_ref[...]
        g_ref[...] = grad
        gg_ref[...] = grad_gain
        df_ref[...] = grad.astype(bf16)
        dacc_ref[...] = jnp.zeros_like(dacc_ref)

    du = (mm(df_ref[...], wo[...]) * gp_ref[...].astype(f32)).astype(bf16)
    du_ref[...] = du
    dacc_ref[...] += mm(du, wi[...], NT)

    @pl.when(step == pl.num_programs(0) - 1)
    def _():
        dn_ref[...] = dacc_ref[...].astype(bf16)


def ffn_bwd(sc, x, dm, mine, other, gain, r, gp, w2, chunk=512):
    rows, width = x.shape
    hidden = w2.shape[1] // 2
    count, stream, first, second, part = ffn_specs(rows, width, hidden, chunk)
    return call(
        ffn_bwd_kernel,
        (count,),
        [SMEM_SPEC, stream, stream, whole(mine.shape), whole(mine.shape), whole(gain.shape)]
        + [part, part, first, second],
        [stream, stream, part, stream, whole(gain.shape)],
        [
            jax.ShapeDtypeStruct((rows, width), f32),
            jax.ShapeDtypeStruct((rows, width), bf16),
            jax.ShapeDtypeStruct((rows, hidden), bf16),
            jax.ShapeDtypeStruct((rows, width), bf16),
            jax.ShapeDtypeStruct(gain.shape, f32),
        ],
        [pltpu.VMEM((width, rows), f32), pltpu.VMEM((rows, width), f32)],
    )(sc, x, dm, mine, other, gain, r, gp, w2, w2)


def last_kernel(sc, x_ref, dm_ref, mine, other, gain, g_ref, gg_ref, joined):
    grad, grad_gain = norm_back(x_ref[...], gain[...], join_halves(sc, mine, other, joined))
    joined_rows = g_ref.shape[0]
    full = grad + dm_ref[...]
    gg_ref[...] = grad_gain
    g_ref[...] = jnp.where(sc[1] == 0, full[:joined_rows], full[joined_rows:]).astype(bf16)


def last_back(sc, x, dm, mine, other, gain):
    rows, width = x.shape
    stream = whole((rows, width))
    return call(
        last_kernel,
        (1,),
        [SMEM_SPEC, stream, stream, whole(mine.shape), whole(mine.shape), whole(gain.shape)],
        [whole((rows // 2, width)), whole(gain.shape)],
        [
            jax.ShapeDtypeStruct((rows // 2, width), bf16),
            jax.ShapeDtypeStruct(gain.shape, f32),
        ],
        [pltpu.VMEM((width, rows), f32)],
    )(sc, x, dm, mine, other, gain)


def join_kernel(sc, m_ref, own, oth, gain, x_ref, mine_ref, other_ref):
    stream = m_ref[...] + (own[...].astype(f32) + oth[...].astype(f32))
    x_ref[...] = stream
    normed = (stream * row_scale(stream) * gain[...]).astype(bf16)
    half = normed.shape[0] // 2
    first = sc[1] == 0
    mine_ref[...] = jnp.where(first, normed[:half], normed[half:])
    other_ref[...] = jnp.where(first, normed[half:], normed[:half])


def join(sc, m, own, oth, gain):
    rows, width = m.shape
    stream = whole((rows, width))
    return call(
        join_kernel,
        (1,),
        [SMEM_SPEC, stream, stream, stream, whole(gain.shape)],
        [stream, whole((rows // 2, width)), whole((rows // 2, width))],
        [
            jax.ShapeDtypeStruct((rows, width), f32),
            jax.ShapeDtypeStruct((rows // 2, width), bf16),
            jax.ShapeDtypeStruct((rows // 2, width), bf16),
        ],
    )(sc, m, own, oth, gain)


def attn_bwd_kernel(
    sc, g_ref, m_ref, own, oth, gain, w_ref, q_ref, kv_ref, e_ref, c32_ref, rl_ref,
    dm_ref, da_ref, dq_ref, dkv_ref, near_ref, far_ref, gg_ref, keep_ref, send_ref,
    dcs_ref, dot_ref, pad_ref,
    *, pieces, rows, inner,
):
    step = pl.program_id(0)
    block = sc[0]
    core = sc[1]
    total = rows * pieces
    width = m_ref.shape[1]
    bands = rows // LANES

    @pl.when(step == 0)
    def _():
        grad_normed = own[...].astype(f32) + oth[...].astype(f32)
        back, grad_gain = norm_back(m_ref[...], gain[...], grad_normed)
        grad = g_ref[...] + back
        dm_ref[...] = grad
        gg_ref[...] = grad_gain
        low_grad = grad.astype(bf16)
        da_ref[...] = low_grad
        scaled = (mm(low_grad, w_ref[:, 3 * inner : 4 * inner]) * rl_ref[...]).astype(bf16)
        dcs_ref[...] = scaled
        dot_ref[...] = scaled.astype(f32) * c32_ref[...]
        zero = jnp.zeros((rows, LANES), bf16)
        pad_ref[:, :LANES] = zero
        pad_ref[:, LANES + total :] = zero

    lane = pl.multiple_of(step * LANES, LANES)
    low = lax.broadcasted_iota(jnp.int32, (rows, LANES), 1) < LANES // 2
    queries = q_ref[:, pl.ds(lane, LANES)]
    keys = kv_ref[:, pl.ds(lane, LANES)]
    values = kv_ref[:, pl.ds(pl.multiple_of(inner + step * LANES, LANES), LANES)]
    columns = lax.broadcasted_iota(jnp.int32, (total, LANES), 0) // LANES
    marks = lax.broadcasted_iota(jnp.int32, (total, LANES), 1) == columns
    keys = jnp.concatenate([keys, marks.astype(bf16)], axis=1)
    scaled = dcs_ref[:, pl.ds(lane, LANES)]
    products = dot_ref[:, pl.ds(lane, LANES)]
    key_sum = None
    value_sum = None
    query_parts = []
    for h in range(2):
        keep = low if h == 0 else ~low
        picked = jnp.where(keep, scaled, jnp.zeros_like(scaled))
        inner_sum = jnp.sum(jnp.where(keep, products, 0.0), axis=-1, keepdims=True)
        weights = e_ref[h]
        grad_probs = mm(picked, values, NT)
        grad_scores = (weights.astype(f32) * (grad_probs - inner_sum)).astype(bf16)
        pad_ref[:, LANES : LANES + total] = grad_scores
        query_grad = mm(grad_scores, keys)
        query_parts.append(query_grad[:, :LANES])
        for i in range(bands):
            far_ref[h, i : i + 1, :] = jnp.sum(
                query_grad[i * LANES : (i + 1) * LANES, LANES:], axis=0, keepdims=True
            )
        near = None
        for i in range(bands):
            start = pl.multiple_of((block * bands + i) * LANES, LANES)
            window = pad_ref[i * LANES : (i + 1) * LANES, pl.ds(start, 3 * LANES)].astype(f32)
            near = window if near is None else near + window
        near_ref[h] = near
        picked_q = jnp.where(keep, queries, jnp.zeros_like(queries))
        key_part = mm(picked_q, grad_scores, TN)
        value_part = mm(picked, weights, TN)
        key_sum = key_part if key_sum is None else key_sum + key_part
        value_sum = value_part if value_sum is None else value_sum + value_part
    dq_ref[:, pl.ds(lane, LANES)] = jnp.where(low, query_parts[0], query_parts[1]).astype(bf16)
    dkv_ref[pl.ds(lane, LANES), :] = key_sum.astype(bf16)
    dkv_ref[pl.ds(pl.multiple_of(inner + step * LANES, LANES), LANES), :] = value_sum.astype(bf16)

    @pl.when(step == pl.num_programs(0) - 1)
    def _():
        part = width // 2
        for side, target in ((core, keep_ref), (1 - core, send_ref)):
            first = pl.multiple_of(side * part, part)
            from_queries = mm(w_ref[pl.ds(first, part), :inner], dq_ref[...], NT)
            weights = w_ref[pl.ds(first, part), inner : 3 * inner]
            for k in range(pieces):
                start = pl.multiple_of((block ^ k) * rows, rows)
                piece = mm(weights, dkv_ref[:, pl.ds(start, rows)])
                if k == 0:
                    piece = piece + from_queries
                target[k] = piece.astype(bf16)


def attn_bwd(sc, g, m, own, oth, gain, w1, q, kv, e, c32, rl):
    rows, width = m.shape
    total = kv.shape[0]
    pieces = total // rows
    inner = q.shape[1]
    heads = e.shape[0]
    bands = rows // LANES
    stream = whole((rows, width))
    pair = pl.BlockSpec((2, rows, total), lambda p: (p, 0, 0))
    shapes = [
        ((rows, width), f32),
        ((rows, width), bf16),
        ((rows, inner), bf16),
        ((2 * inner, total), bf16),
        ((heads, LANES, 3 * LANES), f32),
        ((heads, bands, LANES), f32),
        (gain.shape, f32),
        ((pieces, width // 2, rows), bf16),
        ((pieces, width // 2, rows), bf16),
    ]
    out_specs = [whole(s) for s, _ in shapes]
    out_specs[4] = pl.BlockSpec((2, LANES, 3 * LANES), lambda p: (p, 0, 0))
    out_specs[5] = pl.BlockSpec((2, bands, LANES), lambda p: (p, 0, 0))
    return call(
        functools.partial(attn_bwd_kernel, pieces=pieces, rows=rows, inner=inner),
        (heads // 2,),
        [SMEM_SPEC, stream, stream, stream, stream, whole(gain.shape), whole(w1.shape)]
        + [whole(q.shape), whole(kv.shape), pair, whole(c32.shape), whole(rl.shape)],
        out_specs,
        [jax.ShapeDtypeStruct(s, d) for s, d in shapes],
        [
            pltpu.VMEM((rows, inner), bf16),
            pltpu.VMEM((rows, inner), f32),
            pltpu.VMEM((rows, total + 2 * LANES), bf16),
        ],
    )(sc, g, m, own, oth, gain, w1, q, kv, e, c32, rl)


def ffn_grad_kernel(*refs, slots, count, has_acc, out_dtype):
    n2 = refs[:slots]
    du = refs[slots : 2 * slots]
    df = refs[2 * slots : 3 * slots]
    act = refs[3 * slots : 4 * slots]
    acc = refs[4 * slots] if has_acc else None
    out_ref = refs[-1]
    step = pl.program_id(0)

    def total(left, right):
        value = acc[...] if has_acc else None
        for s in range(slots):
            part = mm(left[s][...], right[s][...], TN)
            value = part if value is None else value + part
        out_ref[...] = value.astype(out_dtype)

    @pl.when(step < count)
    def _():
        total(n2, du)

    @pl.when(step >= count)
    def _():
        total(df, act)


def ffn_grad(n2, du, df, act, acc, out_dtype, chunk=512):
    slots = len(n2)
    rows, width = n2[0].shape
    hidden = du[0].shape[1]
    count = hidden // chunk
    stream = whole((rows, width))
    first = pl.BlockSpec((rows, chunk), lambda j: (0, jnp.minimum(j, count - 1)))
    second = pl.BlockSpec((rows, chunk), lambda j: (0, jnp.maximum(j - count, 0)))
    tile = pl.BlockSpec((width, chunk), lambda j: (0, j))
    args = [*n2, *du, *df, *act]
    specs = [stream] * slots + [first] * slots + [stream] * slots + [second] * slots
    if acc is not None:
        args.append(acc)
        specs.append(tile)
    return call(
        functools.partial(
            ffn_grad_kernel,
            slots=slots, count=count, has_acc=acc is not None, out_dtype=out_dtype,
        ),
        (2 * count,),
        specs,
        tile,
        jax.ShapeDtypeStruct((width, 2 * hidden), out_dtype),
    )(*args)


def attn_grad_kernel(*refs, slots, has_acc, out_dtype):
    sc = refs[0]
    n1 = refs[1 : 1 + slots]
    dq = refs[1 + slots : 1 + 2 * slots]
    dkv = refs[1 + 2 * slots : 1 + 3 * slots]
    da = refs[1 + 3 * slots : 1 + 4 * slots]
    ctx = refs[1 + 4 * slots : 1 + 5 * slots]
    acc = refs[1 + 5 * slots] if has_acc else None
    out_ref = refs[-1]
    step = pl.program_id(0)
    rows = dq[0].shape[0]

    def store(value):
        if has_acc:
            value = value + acc[...]
        out_ref[...] = value.astype(out_dtype)

    def summed(parts):
        value = parts[0]
        for part in parts[1:]:
            value = value + part
        return value

    @pl.when(step == 0)
    def _():
        own = pl.ds(pl.multiple_of(sc[0] * rows, rows), rows)
        store(summed([mm(n1[s][own, :], dq[s][...], TN) for s in range(slots)]))

    @pl.when((step == 1) | (step == 2))
    def _():
        store(summed([mm(dkv[s][...], n1[s][...]) for s in range(slots)]).T)

    @pl.when(step == 3)
    def _():
        store(summed([mm(da[s][...], ctx[s][...], TN) for s in range(slots)]))


def attn_grad(sc, n1, dq, dkv, da, ctx, acc, out_dtype):
    slots = len(n1)
    total, width = n1[0].shape
    rows, inner = dq[0].shape
    tile = pl.BlockSpec((width, inner), lambda j: (0, j))
    half = pl.BlockSpec((inner, total), lambda j: (jnp.clip(j - 1, 0, 1), 0))
    specs = (
        [SMEM_SPEC]
        + [whole((total, width))] * slots
        + [whole((rows, inner))] * slots
        + [half] * slots
        + [whole((rows, width))] * slots
        + [whole((rows, inner))] * slots
    )
    args = [sc, *n1, *dq, *dkv, *da, *ctx]
    if acc is not None:
        args.append(acc)
        specs.append(tile)
    return call(
        functools.partial(
            attn_grad_kernel, slots=slots, has_acc=acc is not None, out_dtype=out_dtype
        ),
        (4,),
        specs,
        tile,
        jax.ShapeDtypeStruct((width, 4 * inner), out_dtype),
    )(*args)


def near_kernel(*refs):
    out_ref = refs[-1]
    near = refs[0][0]
    for ref in refs[1:-1]:
        near = near + ref[0]
    rows, width = near.shape
    relative = (
        lax.broadcasted_iota(jnp.int32, (rows, width), 1)
        - lax.broadcasted_iota(jnp.int32, (rows, width), 0)
        - LANES
    )
    bucket_idx = bucket_of(relative)
    for b in range(NB):
        line = jnp.sum(jnp.where(bucket_idx == b, near, 0.0), axis=0, keepdims=True)
        out_ref[0, b : b + 1, :] = (
            line[:, :LANES] + line[:, LANES : 2 * LANES] + line[:, 2 * LANES :]
        )


def near_sums(parts):
    heads, rows, width = parts[0].shape
    spec = pl.BlockSpec((1, rows, width), lambda h: (h, 0, 0))
    return call(
        near_kernel,
        (heads,),
        [spec] * len(parts),
        pl.BlockSpec((1, NB, LANES), lambda h: (h, 0, 0)),
        jax.ShapeDtypeStruct((heads, NB, LANES), f32),
    )(*parts)


def body(
    tokens, lengths, cotangent, norm_attn, w_query, w_key, w_value, w_attn_out,
    bias_table, norm_ffn, w_ffn_in, w_ffn_out, *, shard_count, context_count,
):
    slots, rows, width = tokens.shape
    half = rows // 2
    pieces = context_count
    total = rows * pieces
    inner = w_query.shape[1]
    heads = bias_table.shape[1]
    shard_rows = w_query.shape[0]
    core = lax.axis_index("tensor")
    context = lax.axis_index("context")
    planes = shard_count == 4 and context_count == 4

    def swap(value):
        return lax.ppermute(value, "tensor", [(0, 1), (1, 0)])

    if planes:
        shard = lax.axis_index("shard")
        block = 2 * (shard % 2) + context % 2
        places = [(y, x, z) for y in range(2) for x in range(2) for z in range(4)]

        def flat(y, x, z):
            return (2 * y + x) * 4 + z

        def moved(y, x, z):
            if x == 0 and z >= 2:
                return flat(y, 1, z - 2)
            if x == 1 and z < 2:
                return flat(y, 0, z + 2)
            return flat(y, x, z)

        home_pairs = [(flat(*p), moved(*p)) for p in places]

        def home(value):
            return lax.ppermute(value, ("shard", "context"), home_pairs)

        def exchange(value, k):
            pairs = [(flat(y, x, z), flat(y, x ^ (k >> 1), z ^ (k & 1))) for y, x, z in places]
            return lax.ppermute(value, ("shard", "context"), pairs)

    else:
        block = context

        def home(value):
            return value

        def exchange(value, k):
            pairs = [(i, i ^ k) for i in range(context_count)]
            return lax.ppermute(value, "context", pairs)

    def ordered(mine, other):
        first = core == 0
        return jnp.concatenate(
            [jnp.where(first, mine, other), jnp.where(first, other, mine)], axis=0
        )

    lens = home(lengths)
    scalars = [
        jnp.stack([block, core, lens[s], jnp.zeros_like(core)]).astype(jnp.int32)
        for s in range(slots)
    ]
    row_pos = block * rows + jnp.arange(rows, dtype=jnp.int32)

    mine_tok = lax.dynamic_slice_in_dim(tokens, core * half, half, axis=1)
    mine_cot = lax.dynamic_slice_in_dim(cotangent, core * half, half, axis=1)
    tok_mine = [home(mine_tok[s]) for s in range(slots)]

    small = jnp.zeros((shard_rows, LANES), bf16)
    small = small.at[:, 0].set(norm_attn).at[:, 1].set(norm_ffn)
    small = small.at[: bias_table.shape[0], 2 : 2 + heads].set(bias_table)
    pack1 = jnp.concatenate([w_query, w_key, w_value, w_attn_out.T, small], axis=1)
    pack2 = jnp.concatenate([w_ffn_in, w_ffn_out.T], axis=1)
    w1 = lax.all_gather(pack1, "shard", axis=0, tiled=True)
    w2 = lax.all_gather(pack2, "shard", axis=0, tiled=True)
    small_full = w1[:, 4 * inner :]
    gains = small_full[:, :2].astype(f32).T
    gain_attn = gains[0:1]
    gain_ffn = gains[1:2]
    table = (
        small_full.reshape(shard_count, shard_rows, LANES)[:, : NB // shard_count, 2 : 2 + heads]
        .reshape(NB, heads)
        .astype(f32)
    )
    offsets = jnp.arange(total + rows, dtype=jnp.int32) - block * rows - (rows - 1)
    hot = (bucket_of(offsets)[None, :] == jnp.arange(NB, dtype=jnp.int32)[:, None]).astype(f32)
    vec = lax.dot_general(
        table, hot, (((0,), (0,)), ((), ())), precision=lax.Precision.HIGHEST
    )
    bias = bias_tile(vec, rows, total)

    def gather(mine):
        got = [mine] + [exchange(mine, k) for k in range(1, pieces)]
        return got

    saved1 = []
    x0 = []
    for s in range(slots):
        mine = gather(tok_mine[s])
        other = [swap(v) for v in mine]
        x0.append(ordered(mine[0], other[0]).astype(f32))
        saved1.append(attn_fwd(scalars[s], mine, other, gain_attn, w1, bias, True))
    x1, mid1, ffn1, saved2 = [], [], [], []
    for s in range(slots):
        part = saved1[s][7]
        m, n2, r, gp, b = ffn_fwd(x0[s], part, swap(part), gain_ffn, w2)
        mid1.append(m)
        ffn1.append((n2, r, gp))
        x, mine, other = join(scalars[s], m, b, swap(b), gain_attn)
        x1.append(x)
        mine = gather(mine)
        other = [other] + [swap(v) for v in mine[1:]]
        saved2.append(attn_fwd(scalars[s], mine, other, gain_attn, w1, bias, False))

    cot = []
    for s in range(slots):
        mine = home(mine_cot[s])
        full = ordered(mine, swap(mine))
        cot.append(jnp.where((row_pos < lens[s])[:, None], full, jnp.zeros_like(full)))
    ffn2 = []
    outs = []
    for s in range(slots):
        part = saved2[s][7]
        m, n2, r, du, b, dn = ffn_both(x1[s], part, swap(part), gain_ffn, cot[s], w2)
        ffn2.append((m, n2, r, du, dn))
        x2 = m + (b.astype(f32) + swap(b).astype(f32))
        x2 = jnp.where((row_pos < lens[s])[:, None], x2, 0.0).astype(bf16)
        mine = home(lax.dynamic_slice_in_dim(x2, core * half, half, axis=0))
        outs.append(ordered(mine, swap(mine)))

    def spread_back(keep, send):
        got = swap(send)
        sums = [keep[k].astype(f32) + got[k].astype(f32) for k in range(pieces)]
        value = sums[0]
        for k in range(1, pieces):
            value = value + exchange(sums[k].astype(bf16), k).astype(f32)
        mine = value.astype(bf16)
        return mine, swap(mine)

    near, far, gain_grads_attn, gain_grads_ffn = [], [], [], []

    def attention_back(s, grad, m, dn, saved):
        dm, da, dq, dkv, near_s, far_s, gg, keep, send = attn_bwd(
            scalars[s], grad, m, dn, swap(dn), gain_ffn, w1,
            saved[1], saved[2], saved[3], saved[4], saved[5],
        )
        near.append(near_s)
        far.append(far_s)
        gain_grads_ffn.append(gg)
        mine, other = spread_back(keep, send)
        return dm, (da, dq, dkv), mine, other

    back2 = []
    for s in range(slots):
        m, n2, r, du, dn = ffn2[s]
        back2.append(attention_back(s, cot[s].astype(f32), m, dn, saved2[s]))
    acc2 = ffn_grad(
        [v[1] for v in ffn2], [v[3] for v in ffn2], cot, [v[2] for v in ffn2], None, f32
    )
    acc1 = attn_grad(
        scalars[0],
        [v[0] for v in saved2],
        [v[1][1] for v in back2],
        [v[1][2] for v in back2],
        [v[1][0] for v in back2],
        [v[6] for v in saved2],
        None,
        f32,
    )

    mid_grads = []
    for s in range(slots):
        dm, _, mine, other = back2[s]
        n2, r, gp = ffn1[s]
        g1, df, du, dn, gg = ffn_bwd(scalars[s], x1[s], dm, mine, other, gain_attn, r, gp, w2)
        gain_grads_attn.append(gg)
        mid_grads.append((g1, df, du, dn))
    grad2 = ffn_grad(
        [v[0] for v in ffn1],
        [v[2] for v in mid_grads],
        [v[1] for v in mid_grads],
        [v[1] for v in ffn1],
        acc2,
        bf16,
    )
    part2 = lax.psum_scatter(grad2, "shard", scatter_dimension=0, tiled=True)
    sum2 = lax.psum(part2, "context").astype(f32)
    back1 = []
    for s in range(slots):
        g1, df, du, dn = mid_grads[s]
        back1.append(attention_back(s, g1, mid1[s], dn, saved1[s]))
    grad1 = attn_grad(
        scalars[0],
        [v[0] for v in saved1],
        [v[1][1] for v in back1],
        [v[1][2] for v in back1],
        [v[1][0] for v in back1],
        [v[6] for v in saved1],
        acc1,
        bf16,
    )
    grad_tokens = []
    for s in range(slots):
        dm, _, mine, other = back1[s]
        g, gg = last_back(scalars[s], x0[s], dm, mine, other, gain_attn)
        gain_grads_attn.append(gg)
        g = home(g)
        grad_tokens.append(ordered(g, swap(g)).astype(f32))

    near_total = jnp.sum(near_sums(near), axis=-1)
    far_total = far[0]
    for value in far[1:]:
        far_total = far_total + value
    bands = rows // LANES
    band = block * bands + jnp.arange(bands, dtype=jnp.int32)[:, None]
    column = jnp.arange(LANES, dtype=jnp.int32)[None, :]
    left = jnp.sum(jnp.where(column < band - 1, far_total, 0.0), axis=(1, 2))
    right = jnp.sum(jnp.where(column > band + 1, far_total, 0.0), axis=(1, 2))
    bucket_ids = jnp.arange(NB, dtype=jnp.int32)[None, :]
    grad_table = (
        near_total
        + jnp.where(bucket_ids == NB // 2 - 1, left[:, None], 0.0)
        + jnp.where(bucket_ids == NB - 1, right[:, None], 0.0)
    ).T
    gain_attn_grad = sum(gain_grads_attn[1:], gain_grads_attn[0])
    gain_ffn_grad = sum(gain_grads_ffn[1:], gain_grads_ffn[0])
    table_rows = NB // shard_count
    table_part = jnp.pad(
        grad_table.reshape(shard_count, table_rows, heads),
        ((0, 0), (0, shard_rows - table_rows), (0, 0)),
    ).reshape(width, heads)
    small_grad = jnp.concatenate([gain_attn_grad.T, gain_ffn_grad.T, table_part], axis=1)
    small_grad = jnp.pad(small_grad, ((0, 0), (0, LANES - small_grad.shape[1])))
    grad1 = jnp.concatenate([grad1, small_grad.astype(bf16)], axis=1)
    part1 = lax.psum_scatter(grad1, "shard", scatter_dimension=0, tiled=True)
    sum1 = lax.psum(part1, "context").astype(f32)
    hidden = w_ffn_in.shape[1]
    return (
        jnp.stack(outs),
        jnp.stack(grad_tokens),
        sum1[:, 4 * inner],
        sum1[:, :inner],
        sum1[:, inner : 2 * inner],
        sum1[:, 2 * inner : 3 * inner],
        sum1[:, 3 * inner : 4 * inner].T,
        sum1[:table_rows, 4 * inner + 2 : 4 * inner + 2 + heads],
        sum1[:, 4 * inner + 1],
        sum2[:, :hidden],
        sum2[:, hidden:].T,
    )


def solution(mesh):
    return jax.shard_map(
        functools.partial(
            body, shard_count=mesh.shape["shard"], context_count=mesh.shape["context"]
        ),
        mesh=mesh,
        in_specs=(
            P("shard", "context", None),
            P("shard"),
            P("shard", "context", None),
            P("shard"),
            P("shard", "tensor"),
            P("shard", "tensor"),
            P("shard", "tensor"),
            P("tensor", "shard"),
            P("shard", "tensor"),
            P("shard"),
            P("shard", "tensor"),
            P("tensor", "shard"),
        ),
        out_specs=(
            P("shard", "context", None),
            P("shard", "context", None),
            P("shard"),
            P("shard", "tensor"),
            P("shard", "tensor"),
            P("shard", "tensor"),
            P("tensor", "shard"),
            P("shard", "tensor"),
            P("shard"),
            P("shard", "tensor"),
            P("tensor", "shard"),
        ),
        check_vma=False,
    )
```
